512 devices in a mesh: src: 32 (over x, y_lo, core), rcv: 16 (over z, y_hi).
Axes of the slice: x: 4, y: 8 (y_hi: 2, y_lo: 4; y = y_hi * 4 + y_lo), z: 8, core: 2. Of those that a mesh axis runs over, the one named last changes fastest.
Arguments:
- traces: float32 [2, 2, 4096, 8192], P(None, None, 'src', 'rcv'), may hold values from -6 to 6
- tap_table: float32 [8, 2, 2, 15, 64], replicated, may hold values from -1 to 1
- receiver_bins: int32 [8, 8192], replicated, may hold values from 0 to 63
- source_bins: int32 [8, 4096], replicated, may hold values from 0 to 63
Outputs:
- redatumed: float32 [2, 2, 16, 512, 4096], P(None, None, 'rcv', 'src')
The draws below stay inside these ranges and needn't reach their ends.
All inputs are finite; a program needn't handle non-finite values.
Results may differ from the reference program's by a relative error of at most 0.0002.
Values sent between devices are 32-bit elements; how exact they have to be, the bound alone decides.
No kernel may reach another device: no remote copies, remote signals or barrier semaphores. Data moves between devices by JAX's collectives and lax.ppermute only.
A program may use at most 192 MiB of HBM per device.

```python
import math
import jax
import jax.numpy as jnp
from jax import lax

F = 2
TAPS = 15
BINS = 64
STEPS = 8
R_DEV = 512
NSRC = 4096
NRCV = 8192
RTILES = 16


def draw_tap_table(key, part):
    base = jax.random.fold_in(key, 11)
    phase_key, tap_key = jax.random.split(base, 2)
    phases = jax.random.uniform(phase_key, (STEPS, 1, F, 1, BINS), jnp.float32, -math.pi, math.pi)
    others = jnp.clip(0.11 * jax.random.normal(tap_key, (STEPS, 2, F, TAPS, BINS), jnp.float32), -0.6, 0.6)
    centre = 0.8
    middle = jnp.concatenate([centre * jnp.cos(phases), centre * jnp.sin(phases)], axis=1)
    tap_pos = jnp.arange(TAPS)[None, None, None, :, None]
    return jnp.where(tap_pos == (TAPS - 1) // 2, middle, others).astype(jnp.float32)


def with_ends(array, key, least, top_value):
    spot = [jax.random.randint(jax.random.fold_in(key, axis), (), 0, length) for axis, length in enumerate(array.shape)]
    longest = array.shape.index(max(array.shape))
    next_to = spot[:longest] + [(spot[longest] + 1) % array.shape[longest]] + spot[longest + 1:]
    return array.at[tuple(spot)].set(least).at[tuple(next_to)].set(top_value)


def levels(key, shape, shards, least, high):
    level, own = 1.0, jax.random.fold_in(key, 6)
    for dim, blocks in shards:
        steps = jnp.exp(jax.random.uniform(jax.random.fold_in(own, dim), (blocks,), jnp.float32, least / len(shards), high / len(shards)))
        level = level * jnp.repeat(steps, shape[dim] // blocks).reshape([-1 if axis == dim else 1 for axis in range(len(shape))])
    return level


def centred(rng, shape, spread, limit, pieces=(), dtype=jnp.bfloat16):
    loudness = levels(rng, shape, pieces, -0.22, 0.18) if pieces else 1.0
    drawn = jax.random.normal(rng, shape, jnp.float32) * spread * loudness
    return jnp.minimum(jnp.maximum(drawn, -limit), limit).astype(dtype)


def setup_inputs(seed: int = 0) -> dict:
    arg_keys = jax.random.split(jax.random.key(seed), 5)
    return {
        "traces": centred(arg_keys[0], (2, F, NSRC, NRCV), 1.0, 6.0, ((2, 32), (3, 16)), jnp.float32),
        "tap_table": draw_tap_table(jax.random.fold_in(arg_keys[4], 71), 0),
        "receiver_bins": with_ends(jax.random.randint(arg_keys[2], (STEPS, NRCV), 0, BINS), jax.random.fold_in(arg_keys[2], 1), 0, BINS - 1).astype(jnp.int32),
        "source_bins": with_ends(jax.random.randint(arg_keys[3], (STEPS, NSRC), 0, BINS), jax.random.fold_in(arg_keys[3], 1), 0, BINS - 1).astype(jnp.int32),
    }


def apply_taps(padded, taps_now):
    columns = taps_now.shape[3]
    tap_count = taps_now.shape[2]
    last_axis = padded.ndim - 1
    broad_shape = (taps_now.shape[1],) + (1,) * (padded.ndim - 3) + (columns,)

    def add_tap(offset, partial_value):
        real_sum, imag_sum = partial_value
        offset = jnp.asarray(offset).astype(jnp.int32)
        window = lax.dynamic_slice_in_dim(padded, offset, columns, last_axis)
        tap_both = lax.dynamic_index_in_dim(taps_now, offset, 2, keepdims=False)
        tap_real = tap_both[0].reshape(broad_shape)
        tap_imag = tap_both[1].reshape(broad_shape)
        piece_real = window[0]
        piece_imag = window[1]
        return (real_sum + tap_real * piece_real - tap_imag * piece_imag,
                imag_sum + tap_real * piece_imag + tap_imag * piece_real)

    out_shape = padded.shape[1:-1] + (columns,)
    initial = jnp.zeros(out_shape, jnp.float32)
    real_sum, imag_sum = lax.fori_loop(0, tap_count, add_tap, (initial, initial))
    return jnp.stack([real_sum, imag_sum])


def extrapolate(wavefield, tap_table, bins_all):
    half_span = (TAPS - 1) // 2
    for depth_step in range(STEPS):
        taps_now = tap_table[depth_step][:, :, :, bins_all[depth_step]]
        padded = jnp.pad(wavefield, ((0, 0),) * (wavefield.ndim - 1) + ((half_span, half_span),))
        wavefield = apply_taps(padded, taps_now)
    return wavefield


def reference(traces, tap_table, receiver_bins, source_bins):
    wavefield = extrapolate(traces, tap_table, receiver_bins)
    wavefield = jnp.swapaxes(wavefield, 2, 3)
    wavefield = extrapolate(wavefield, tap_table, source_bins)
    return wavefield.reshape(2, F, RTILES, R_DEV, NSRC)
```

```python
import functools

import jax
import jax.numpy as jnp
from jax import lax
from jax.experimental import pallas as pl
from jax.experimental.pallas import tpu as pltpu
from jax.sharding import PartitionSpec as P

F = 2
TAPS = 15
BINS = 64
STEPS = 8
HALF = 7
MARGIN = HALF * STEPS
TILE = 512
S_DEV = 128
GROUPS = 32
PER = 16
NSRC = GROUPS * S_DEV
OUTS = 112
WIN = 128
BLOCKS = 6
ROWS = 704
PCOLS = 768
RUN = 32
KINDS = 3
TROWS = 48
BF16 = jnp.bfloat16
F32 = jnp.float32
VMEM_LIMIT = 56 * 1024 * 1024


def rounded(x):
    return lax.reduce_precision(x, exponent_bits=8, mantissa_bits=7)


def rcv_taps_kernel(bins_ref, table_ref, out_ref):
    rows = lax.broadcasted_iota(jnp.int32, (BINS, PCOLS), 0)
    lanes = lax.broadcasted_iota(jnp.int32, (1, PCOLS), 1)
    for d in range(STEPS):
        offset = 128 - MARGIN + HALF * (d + 1)
        row = pltpu.roll(bins_ref[d : d + 1, :], PCOLS - offset, axis=1)
        count = TILE + 2 * MARGIN - 2 * HALF * (d + 1)
        row = jnp.where(lanes < count, row, -1)
        onehot = jnp.where(rows == row, 1.0, 0.0).astype(BF16)
        taps = jnp.dot(table_ref[d], onehot, preferred_element_type=F32)
        for i in range(PCOLS // 128):
            out_ref[d, i * 128 : (i + 1) * 128, :] = taps[:, i * 128 : (i + 1) * 128].T


def rcv_taps(window_bins, table):
    return pl.pallas_call(
        rcv_taps_kernel,
        out_shape=jax.ShapeDtypeStruct((STEPS, PCOLS, 128), F32),
        compiler_params=pltpu.CompilerParams(vmem_limit_bytes=VMEM_LIMIT),
        cost_estimate=pl.CostEstimate(flops=200_000_000, bytes_accessed=3_200_000, transcendentals=0),
        name="rcv_taps",
    )(window_bins, table)


def put_split(dst, c, start, size, value):
    hi = value.astype(BF16)
    dst[c, start : start + size, 0:128] = hi
    dst[c, start : start + size, 128:256] = (value - hi.astype(F32)).astype(BF16)


def rcv_kernel(fs, local_ref, low_ref, high_ref, taps_ref, out_ref, first, za, zb, last):
    step = pl.program_id(0)
    n = len(fs)

    @pl.when(step == 0)
    def _():
        for j in range(n):
            for c in range(2):
                first[0:MARGIN, :] = low_ref[c, j]
                for i in range(TILE // 128):
                    base = MARGIN + i * 128
                    first[base : base + 128, :] = local_ref[c, j, :, i * 128 : (i + 1) * 128].T
                first[MARGIN + TILE : 2 * MARGIN + TILE, :] = high_ref[c, j]
                first[2 * MARGIN + TILE :, :] = jnp.zeros((ROWS - 2 * MARGIN - TILE, 128), F32)
                for base in range(0, ROWS, 64):
                    put_split(za.at[j], c, base, 64, first[base : base + 64, :])
                zb[j, c, BLOCKS * OUTS :, :] = jnp.zeros((ROWS - BLOCKS * OUTS, 256), BF16)

    p = lax.broadcasted_iota(jnp.int32, (OUTS, 128), 0)
    lane = lax.broadcasted_iota(jnp.int32, (OUTS, 128), 1)
    band = (lane >= p) & (lane < p + TAPS)

    def unit(src, dst, dd, j, b, keep):
        f = fs[j]
        start = b * OUTS
        w = taps_ref[dd, start : start + OUTS, :]
        parts = []
        for kind in range(4):
            shift = (256 - 64 * f - 16 * kind) % 128
            turned = pltpu.roll(w, shift, axis=1, stride=1, stride_axis=0)
            parts.append(jnp.where(band, turned, 0.0).astype(BF16))
        re_hi, im_hi, re_lo, im_lo = parts
        lhs = jnp.concatenate(
            [
                jnp.concatenate([re_hi, -im_hi], axis=1),
                jnp.concatenate([im_hi, re_hi], axis=1),
                jnp.concatenate([re_lo, -im_lo], axis=1),
                jnp.concatenate([im_lo, re_lo], axis=1),
            ],
            axis=0,
        )
        rhs = jnp.concatenate(
            [src[j, 0, start : start + WIN, :], src[j, 1, start : start + WIN, :]], axis=0
        )
        product = jnp.dot(lhs, rhs, preferred_element_type=F32)
        for c in range(2):
            top = product[c * OUTS : (c + 1) * OUTS]
            low = product[(2 + c) * OUTS : (3 + c) * OUTS]
            value = top[:, :128] + (top[:, 128:] + low[:, :128])
            put_split(dst.at[j], c, start, OUTS, value)
            if keep:
                last[j, c, start : start + OUTS, :] = value

    for b in range(BLOCKS):
        for j in range(n):
            unit(za, zb, 0, j, b, False)
    for b in range(BLOCKS):
        for j in range(n):
            unit(zb, za, 1, j, b, True)

    @pl.when(step == STEPS // 2 - 1)
    def _():
        for j in range(n):
            for c in range(2):
                for g in range(GROUPS):
                    out_ref[g, c, j] = last[j, c, g * PER : (g + 1) * PER, :]


def rcv_steps(fs, local, low, high, taps):
    n = len(fs)
    f0 = fs[0] // n
    return pl.pallas_call(
        functools.partial(rcv_kernel, fs),
        grid=(STEPS // 2,),
        out_shape=jax.ShapeDtypeStruct((GROUPS, 2, n, PER, S_DEV), F32),
        in_specs=[
            pl.BlockSpec((2, n, S_DEV, TILE), lambda i: (0, f0, 0, 0)),
            pl.BlockSpec((2, n, MARGIN, S_DEV), lambda i: (0, f0, 0, 0)),
            pl.BlockSpec((2, n, MARGIN, S_DEV), lambda i: (0, f0, 0, 0)),
            pl.BlockSpec((2, PCOLS, 128), lambda i: (i, 0, 0)),
        ],
        out_specs=pl.BlockSpec((GROUPS, 2, n, PER, S_DEV), lambda i: (0, 0, 0, 0, 0)),
        scratch_shapes=[
            pltpu.VMEM((ROWS, 128), F32),
            pltpu.VMEM((n, 2, ROWS, 256), BF16),
            pltpu.VMEM((n, 2, ROWS, 256), BF16),
            pltpu.VMEM((n, 2, BLOCKS * OUTS, 128), F32),
        ],
        compiler_params=pltpu.CompilerParams(
            vmem_limit_bytes=VMEM_LIMIT, dimension_semantics=("arbitrary",)
        ),
        cost_estimate=pl.CostEstimate(
            flops=n * 2_500_000_000, bytes_accessed=n * 4_000_000, transcendentals=0
        ),
        name="rcv_steps",
    )(local, low, high, taps)


def src_taps_kernel(bins_ref, table_ref, out_ref):
    rows = lax.broadcasted_iota(jnp.int32, (BINS, 128), 0)
    table = table_ref[0]

    def pair(i, carry):
        halves = []
        for h in range(2):
            row = bins_ref[0, pl.ds(2 * i + h, 1), :]
            onehot = jnp.where(rows == row, 1.0, 0.0).astype(BF16)
            halves.append(jnp.concatenate([onehot] * 3, axis=0))
        taps = jnp.dot(table, jnp.concatenate(halves, axis=1), preferred_element_type=F32)
        for h in range(2):
            for f in range(F):
                out_ref[f, 0, 2 * i + h] = taps[f * TROWS : (f + 1) * TROWS, h * 128 : (h + 1) * 128]
        return carry

    lax.fori_loop(0, RUN // 2, pair, 0, unroll=4)


def src_taps(bins, table):
    return pl.pallas_call(
        src_taps_kernel,
        grid=(STEPS,),
        out_shape=jax.ShapeDtypeStruct((F, STEPS, RUN, TROWS, 128), F32),
        in_specs=[
            pl.BlockSpec((1, RUN, 128), lambda d: (d, 0, 0)),
            pl.BlockSpec((1, F * TROWS, 3 * BINS), lambda d: (d, 0, 0)),
        ],
        out_specs=pl.BlockSpec((F, 1, RUN, TROWS, 128), lambda d: (0, d, 0, 0, 0)),
        compiler_params=pltpu.CompilerParams(
            vmem_limit_bytes=VMEM_LIMIT, dimension_semantics=("arbitrary",)
        ),
        cost_estimate=pl.CostEstimate(
            flops=1_200_000_000, bytes_accessed=13_000_000, transcendentals=0
        ),
        name="src_taps",
    )(bins, table)


PAD = HALF
MROWS = RUN + 2 * PAD


def src_kernel(n, recv_ref, taps_ref, *rest):
    out_ref, xa, xb, swap, place = rest[-5:]
    step = pl.program_id(0)
    lane = lax.broadcasted_iota(jnp.int32, (RUN, 128), 1)
    quarter = lane // 32
    lane8 = lax.broadcasted_iota(jnp.int32, (PER, 128), 1)

    def choose(pieces):
        out = pieces[3]
        for q in range(3):
            out = jnp.where(quarter == q, pieces[q], out)
        return out

    def turned(x, shift):
        shift %= 128
        return x if shift == 0 else pltpu.roll(x, shift, axis=1)

    def put(dst, j, m, re, im):
        dst[j, 0, m] = re
        dst[j, 1, m] = im
        dst[j, 2, m] = re + im

    def halo(x):
        for j in range(n):
            for m in range(PAD):
                parts = []
                for c in range(2):
                    v = x[j, c, RUN + m]
                    one = jnp.where(lane8 == 0, 0.0, pltpu.roll(v, 33, axis=1))
                    parts.append(jnp.where(lane8 < 32, one, pltpu.roll(v, 32, axis=1)))
                put(x, j, m, *parts)
                parts = []
                for c in range(2):
                    v = x[j, c, PAD + m]
                    one = jnp.where(lane8 == 127, 0.0, pltpu.roll(v, 95, axis=1))
                    parts.append(jnp.where(lane8 >= 96, one, pltpu.roll(v, 96, axis=1)))
                put(x, j, PAD + RUN + m, *parts)

    @pl.when(step == 0)
    def _():
        for j in range(n):
            for c in range(2):
                for a in range(PER // 4):
                    rows = [
                        recv_ref[pl.ds((c * n + j) * PER + 4 * a + r, GROUPS, stride=2 * n * PER), :]
                        for r in range(4)
                    ]
                    t = jnp.concatenate(rows, axis=0).T
                    for r in range(4):
                        pieces = [turned(t[32 * q : 32 * q + 32], 32 * (q - r)) for q in range(4)]
                        swap[c, (4 * a + r) * RUN : (4 * a + r + 1) * RUN, :] = choose(pieces)
            for m in range(RUN):
                put(xa, j, PAD + m, *[swap[c, pl.ds(m, PER, stride=RUN), :] for c in range(2)])
        halo(xa)

    MB = 4

    def one_step(src, dst, dd):
        for j in range(n):

            def block(i, carry):
                m0 = i * MB
                seen = {}

                def load(kind, row, rt):
                    key = (kind, row, rt)
                    if key not in seen:
                        seen[key] = src[j, kind, m0 + row, rt * 8 : (rt + 1) * 8, :]
                    return seen[key]

                sums = {}
                for k in range(TAPS):
                    for mm in range(MB):
                        taps = [
                            taps_ref[j, dd, m0 + mm, pl.ds(kind * TAPS + k, 8, stride=0), :]
                            for kind in range(KINDS)
                        ]
                        for rt in range(2):
                            a = load(0, mm + k, rt)
                            b = load(1, mm + k, rt)
                            s = load(2, mm + k, rt)
                            new = [taps[0] * s, taps[1] * a, taps[2] * b]
                            old = sums.get((mm, rt))
                            sums[(mm, rt)] = new if old is None else [x + y for x, y in zip(old, new)]
                for mm in range(MB):
                    for rt in range(2):
                        k1, k2, k3 = sums[(mm, rt)]
                        re = k1 - k3
                        im = k1 + k2
                        at = slice(rt * 8, (rt + 1) * 8)
                        dst[j, 0, PAD + m0 + mm, at, :] = re
                        dst[j, 1, PAD + m0 + mm, at, :] = im
                        dst[j, 2, PAD + m0 + mm, at, :] = re + im
                return carry

            lax.fori_loop(0, RUN // MB, block, 0)

    one_step(xa, xb, 0)
    halo(xb)
    one_step(xb, xa, 1)
    halo(xa)

    @pl.when(step == STEPS // 2 - 1)
    def _():
        for j in range(n):
            for c in range(2):
                for m in range(RUN):
                    swap[c, pl.ds(m, PER, stride=RUN), :] = xa[j, c, PAD + m]
                for a in range(PER // 4):
                    rows = [
                        swap[c, (4 * a + r) * RUN : (4 * a + r + 1) * RUN, :] for r in range(4)
                    ]
                    t = jnp.concatenate(
                        [
                            choose([turned(rows[r], 32 * (r - q)) for r in range(4)])
                            for q in range(4)
                        ],
                        axis=0,
                    ).T
                    for r in range(4):
                        at = 4 * a + r
                        place[at // 8, pl.ds(at % 8, GROUPS, stride=8), :] = t[32 * r : 32 * r + 32]
                for rt in range(2):
                    for i in range(GROUPS):
                        out_ref[c, j, 0, rt * 8 : (rt + 1) * 8, i * 128 : (i + 1) * 128] = place[
                            rt, i * 8 : (i + 1) * 8, :
                        ]


def src_steps(fs, received, taps, earlier=None):
    n = len(fs)
    f0 = fs[0] // n
    flat = received.reshape(GROUPS * 2 * n * PER, S_DEV)
    in_specs = [
        pl.BlockSpec((GROUPS * 2 * n * PER, S_DEV), lambda i: (0, 0)),
        pl.BlockSpec((n, 2, RUN, TROWS, 128), lambda i: (f0, i, 0, 0, 0)),
    ]
    args = [flat, taps]
    aliases = {}
    if earlier is not None:
        in_specs.append(pl.BlockSpec(memory_space=pl.ANY))
        args.append(earlier)
        aliases = {2: 0}
    return pl.pallas_call(
        functools.partial(src_kernel, n),
        grid=(STEPS // 2,),
        out_shape=jax.ShapeDtypeStruct((2, F, 1, PER, NSRC), F32),
        in_specs=in_specs,
        out_specs=pl.BlockSpec((2, n, 1, PER, NSRC), lambda i: (0, f0, 0, 0, 0)),
        scratch_shapes=[
            pltpu.VMEM((n, KINDS, MROWS, PER, 128), F32),
            pltpu.VMEM((n, KINDS, MROWS, PER, 128), F32),
            pltpu.VMEM((2, PER * RUN, 128), F32),
            pltpu.VMEM((2, GROUPS * 8, 128), F32),
        ],
        input_output_aliases=aliases,
        compiler_params=pltpu.CompilerParams(
            vmem_limit_bytes=VMEM_LIMIT, dimension_semantics=("arbitrary",)
        ),
        cost_estimate=pl.CostEstimate(
            flops=n * 3_000_000_000, bytes_accessed=n * 8_000_000, transcendentals=0
        ),
        name="src_steps",
    )(*args)


def rcv_table(tap_table):
    hi = rounded(tap_table)
    lo = rounded(tap_table - hi)
    parts = jnp.concatenate([hi, lo], axis=1)
    parts = jnp.pad(parts, ((0, 0), (0, 0), (0, 0), (0, 1), (0, 0)))
    return parts.transpose(0, 2, 1, 3, 4).reshape(STEPS, F * 4 * 16, BINS).astype(BF16)


def src_table(tap_table):
    re, im = tap_table[:, 0], tap_table[:, 1]
    kinds = jnp.stack([re, im - re, re + im], axis=2)
    flat = kinds.reshape(STEPS, F, KINDS * TAPS, BINS)
    flat = jnp.pad(flat, ((0, 0), (0, 0), (0, TROWS - KINDS * TAPS), (0, 0)))
    flat = flat.reshape(STEPS, F * TROWS, BINS)
    hi = rounded(flat)
    mid = rounded(flat - hi)
    lo = flat - hi - mid
    return jnp.concatenate([hi, mid, lo], axis=2).astype(BF16)


def shards(traces, tap_table, receiver_bins, source_bins):
    count = lax.axis_size("rcv")
    forward = [(i, i + 1) for i in range(count - 1)]
    backward = [(target, source) for source, target in forward]
    tail = traces[:, :, :, TILE - MARGIN :].transpose(0, 1, 3, 2)
    head = traces[:, :, :, :MARGIN].transpose(0, 1, 3, 2)
    low = lax.ppermute(tail, "rcv", forward)
    high = lax.ppermute(head, "rcv", backward)
    padded = jnp.pad(receiver_bins, ((0, 0), (128, 128)), constant_values=-1)
    window = lax.dynamic_slice_in_dim(padded, lax.axis_index("rcv") * TILE, PCOLS, 1)
    r_taps = rcv_taps(window, rcv_table(tap_table))
    s_bins = source_bins.reshape(STEPS, GROUPS, 4, RUN).transpose(0, 3, 2, 1)
    s_taps = src_taps(s_bins.reshape(STEPS, RUN, 128), src_table(tap_table))
    out = None
    for fs in CHUNKS:
        sent = rcv_steps(fs, traces, low, high, r_taps)
        got = lax.all_to_all(sent, "src", split_axis=0, concat_axis=0, tiled=True)
        out = src_steps(fs, got, s_taps, out)
    return out


CHUNKS = ((0, 1),)


def solution(mesh):
    in_specs = (P(None, None, "src", "rcv"), P(), P(), P())
    out_specs = P(None, None, "rcv", "src", None)
    return jax.shard_map(shards, mesh=mesh, in_specs=in_specs, out_specs=out_specs, check_vma=False)
```

```python
import functools

import jax
import jax.numpy as jnp
from jax import lax
from jax.experimental import pallas as pl
from jax.experimental.pallas import tpu as pltpu
from jax.sharding import PartitionSpec as P

F = 2
TAPS = 15
BINS = 64
STEPS = 8
HALF = 7
MARGIN = HALF * STEPS
TILE = 512
S_DEV = 128
GROUPS = 32
PER = 16
NSRC = GROUPS * S_DEV
OUTS = 112
WIN = 128
BLOCKS = 6
ROWS = 704
PCOLS = 768
RUN = 32
KINDS = 3
TROWS = 48
BF16 = jnp.bfloat16
F32 = jnp.float32
MIB = 1024 * 1024


def choose(quarter, pieces):
    out = pieces[3]
    for q in range(3):
        out = jnp.where(quarter == q, pieces[q], out)
    return out


def turned(x, shift):
    shift %= 128
    return x if shift == 0 else pltpu.roll(x, shift, axis=1)


def prepare_kernel(
    tile_ref,
    bins_ref,
    table_ref,
    local_ref,
    source_ref,
    out_ref,
    turned0_ref,
    turned1_ref,
    ordered_ref,
    split_ref,
    tiles,
):
    rows = lax.broadcasted_iota(jnp.int32, (BINS, PCOLS), 0)
    lanes = lax.broadcasted_iota(jnp.int32, (1, PCOLS), 1)
    tile = tile_ref[0]
    total = bins_ref.shape[1]
    start = tile * TILE
    before = pl.multiple_of(jnp.maximum(start - 128, 0), 128)
    after = pl.multiple_of(jnp.minimum(start + TILE, total - 128), 128)
    window = jnp.concatenate(
        [
            jnp.where(tile > 0, bins_ref[:, pl.ds(before, 128)], -1),
            bins_ref[:, pl.ds(pl.multiple_of(start, TILE), TILE)],
            jnp.where(start + TILE < total, bins_ref[:, pl.ds(after, 128)], -1),
        ],
        axis=1,
    )
    blank = jnp.zeros((1, BINS), F32)
    for d in range(STEPS):
        offset = 128 - MARGIN + HALF * (d + 1)
        row = pltpu.roll(window[d : d + 1, :], PCOLS - offset, axis=1)
        count = TILE + 2 * MARGIN - 2 * HALF * (d + 1)
        row = jnp.where(lanes < count, row, -1)
        onehot = jnp.where(rows == row, 1.0, 0.0).astype(BF16)
        parts = []
        for f in range(F):
            pair = [jnp.concatenate([table_ref[d, c, f], blank], axis=0) for c in range(2)]
            his = [x.astype(BF16) for x in pair]
            parts += his + [(x - h.astype(F32)).astype(BF16) for x, h in zip(pair, his)]
        table = jnp.concatenate(parts, axis=0)
        taps = jnp.dot(table, onehot, preferred_element_type=F32)
        for start in range(0, BLOCKS * OUTS, 128):
            size = min(128, BLOCKS * OUTS - start)
            piece = taps[:, start : start + 128].T
            out_ref[d, start : start + size, :] = piece[:size].astype(BF16)
    for f in range(F):
        for c in range(2):
            for i in range(TILE // 128):
                at = slice(i * 128, (i + 1) * 128)
                (turned0_ref, turned1_ref)[f][c, at, :] = local_ref[c, f, :, at].T
    quarter = lax.broadcasted_iota(jnp.int32, (RUN, 128), 1) // 32
    for i in range(GROUPS):
        tiles[i * 8 : (i + 1) * 8, :] = source_ref[:, i * 128 : (i + 1) * 128]
    for half in range(2):
        four = [tiles[pl.ds(4 * half + r, GROUPS, stride=8), :] for r in range(4)]
        t = jnp.concatenate(four, axis=0).T
        for r in range(4):
            pieces = [turned(t[32 * q : 32 * q + 32], 32 * (q - r)) for q in range(4)]
            ordered_ref[4 * half + r] = choose(quarter, pieces)
    unused = jnp.zeros((TROWS, 256 - 3 * BINS), BF16)
    for d in range(STEPS):
        for f in range(F):
            re, im = table_ref[d, 0, f], table_ref[d, 1, f]
            full = jnp.concatenate([re, blank, im - re, blank, re + im, blank], axis=0)
            hi = full.astype(BF16)
            rest = full - hi.astype(F32)
            mid = rest.astype(BF16)
            lo = (rest - mid.astype(F32)).astype(BF16)
            split_ref[f, d] = jnp.concatenate([hi, mid, lo, unused], axis=1)


def prepare(tile, bins, table, local, source_bins):
    vmem = pl.BlockSpec(memory_space=pltpu.VMEM)
    return pl.pallas_call(
        prepare_kernel,
        out_shape=(
            pltpu.VMEM((STEPS, BLOCKS * OUTS, 128), BF16),
            pltpu.VMEM((2, TILE, S_DEV), F32),
            pltpu.VMEM((2, TILE, S_DEV), F32),
            pltpu.HBM((STEPS, RUN, 128), jnp.int32),
            pltpu.HBM((F, STEPS, TROWS, 256), BF16),
        ),
        in_specs=[pl.BlockSpec(memory_space=pltpu.SMEM)] + [vmem] * 4,
        out_specs=(vmem,) * 5,
        scratch_shapes=[pltpu.VMEM((GROUPS * 8, 128), jnp.int32)],
        compiler_params=pltpu.CompilerParams(vmem_limit_bytes=10 * MIB),
        cost_estimate=pl.CostEstimate(flops=200_000_000, bytes_accessed=3_200_000, transcendentals=0),
        name="prepare",
    )(tile, bins, table, local, source_bins)


def put_split(dst, c, start, size, value):
    hi = value.astype(BF16)
    dst[c, start : start + size, 0:128] = hi
    dst[c, start : start + size, 128:256] = (value - hi.astype(F32)).astype(BF16)


def rcv_kernel(f, local_ref, low_ref, high_ref, taps_ref, *rest):
    out_ref, first, za, zb, last = rest[-5:]
    for c in range(2):
        first[0:MARGIN, :] = low_ref[c, f]
        first[MARGIN : MARGIN + TILE, :] = local_ref[c]
        first[MARGIN + TILE : 2 * MARGIN + TILE, :] = high_ref[c, f]
        first[2 * MARGIN + TILE :, :] = jnp.zeros((ROWS - 2 * MARGIN - TILE, 128), F32)
        for base in range(0, ROWS, 64):
            put_split(za, c, base, 64, first[base : base + 64, :])
        zb[c, BLOCKS * OUTS :, :] = jnp.zeros((ROWS - BLOCKS * OUTS, 256), BF16)

    p = lax.broadcasted_iota(jnp.int32, (OUTS, 128), 0)
    lane = lax.broadcasted_iota(jnp.int32, (OUTS, 128), 1)
    band = (lane >= p) & (lane < p + TAPS)

    def unit(src, dst, d, b, keep):
        start = b * OUTS
        w = taps_ref[d, start : start + OUTS, :].astype(F32)
        parts = []
        for kind in range(4):
            shift = (256 - 64 * f - 16 * kind) % 128
            turned = pltpu.roll(w, shift, axis=1, stride=1, stride_axis=0)
            parts.append(jnp.where(band, turned, 0.0).astype(BF16))
        re_hi, im_hi, re_lo, im_lo = parts
        lhs = jnp.concatenate(
            [
                jnp.concatenate([re_hi, -im_hi], axis=1),
                jnp.concatenate([im_hi, re_hi], axis=1),
                jnp.concatenate([re_lo, -im_lo], axis=1),
                jnp.concatenate([im_lo, re_lo], axis=1),
            ],
            axis=0,
        )
        rhs = jnp.concatenate(
            [src[0, start : start + WIN, :], src[1, start : start + WIN, :]], axis=0
        )
        product = jnp.dot(lhs, rhs, preferred_element_type=F32)
        for c in range(2):
            top = product[c * OUTS : (c + 1) * OUTS]
            low = product[(2 + c) * OUTS : (3 + c) * OUTS]
            value = top[:, :128] + (top[:, 128:] + low[:, :128])
            put_split(dst, c, start, OUTS, value)
            if keep:
                last[c, start : start + OUTS, :] = value

    def two_steps(i, blocks):
        for b in range(blocks):
            unit(za, zb, 2 * i, b, False)
        for b in range(blocks):
            unit(zb, za, 2 * i + 1, b, True)

    lax.fori_loop(0, 2, lambda i, _: (two_steps(i, BLOCKS), 0)[1], 0)
    lax.fori_loop(2, 4, lambda i, _: (two_steps(i, BLOCKS - 1), 0)[1], 0)
    for c in range(2):
        for g in range(GROUPS):
            out_ref[g, c, 0] = last[c, g * PER : (g + 1) * PER, :]


def rcv_steps(f, local, low, high, taps, *tokens):
    vmem = pl.BlockSpec(memory_space=pltpu.VMEM)
    return pl.pallas_call(
        functools.partial(rcv_kernel, f),
        out_shape=pltpu.HBM((GROUPS, 2, 1, PER, S_DEV), F32),
        in_specs=[vmem] * 4 + [pl.BlockSpec(memory_space=pl.ANY)] * len(tokens),
        out_specs=vmem,
        scratch_shapes=[
            pltpu.VMEM((ROWS, 128), F32),
            pltpu.VMEM((2, ROWS, 256), BF16),
            pltpu.VMEM((2, ROWS, 256), BF16),
            pltpu.VMEM((2, BLOCKS * OUTS, 128), F32),
        ],
        compiler_params=pltpu.CompilerParams(vmem_limit_bytes=10 * MIB),
        cost_estimate=pl.CostEstimate(
            flops=2_500_000_000, bytes_accessed=4_000_000, transcendentals=0
        ),
        name="rcv_steps",
    )(local, low, high, taps, *tokens)


def look_up(dst, row_of, table, m0):
    which = lax.broadcasted_iota(jnp.int32, (BINS, 128), 0)
    halves = []
    for h in range(2):
        onehot = jnp.where(which == row_of(m0 + h), 1.0, 0.0).astype(BF16)
        halves.append(jnp.concatenate([onehot] * 3, axis=0))
    taps = jnp.dot(table, jnp.concatenate(halves, axis=1), preferred_element_type=F32)
    for h in range(2):
        dst[m0 + h] = taps[:, h * 128 : (h + 1) * 128]


def src_taps_kernel(bins_ref, table_ref, out_ref, token_ref):
    token_ref[...] = jnp.zeros_like(token_ref)
    for i in range(RUN // 2):
        look_up(
            out_ref.at[0],
            lambda m: bins_ref[0, m : m + 1, :],
            table_ref[0, 0, :, : KINDS * BINS],
            2 * i,
        )


def src_taps(f, bins, table):
    return pl.pallas_call(
        src_taps_kernel,
        grid=(STEPS,),
        out_shape=(
            pltpu.HBM((STEPS, RUN, TROWS, 128), F32),
            pltpu.HBM((8, 128), F32),
        ),
        in_specs=[
            pl.BlockSpec((1, RUN, 128), lambda d: (d, 0, 0)),
            pl.BlockSpec((1, 1, TROWS, 256), lambda d: (f, d, 0, 0)),
        ],
        out_specs=(
            pl.BlockSpec((1, RUN, TROWS, 128), lambda d: (d, 0, 0, 0)),
            pl.BlockSpec((8, 128), lambda d: (0, 0)),
        ),
        compiler_params=pltpu.CompilerParams(
            vmem_limit_bytes=8 * MIB, dimension_semantics=("arbitrary",)
        ),
        cost_estimate=pl.CostEstimate(
            flops=1_200_000_000, bytes_accessed=13_000_000, transcendentals=0
        ),
        name="src_taps",
    )(bins, table)


PAD = HALF
MROWS = RUN + 2 * PAD


MB = 2


NSCRATCH = {True: 12, False: 9}


def src_kernel(f, inline, recv_ref, bins_ref, table_ref, *rest):
    out_ref, xa, xb, swap, place, stage, sems, in_sems, *looked = rest[1 if len(rest) > NSCRATCH[inline] else 0 :]
    if inline:
        wa, wb, bins, table = looked
    else:
        (held,) = looked
        wa = wb = None

    if inline:
        first = [
            pltpu.make_async_copy(bins_ref, bins, in_sems.at[0]),
            pltpu.make_async_copy(table_ref.at[f], table, in_sems.at[1]),
        ]
    else:
        first = [
            pltpu.make_async_copy(bins_ref.at[d], held.at[d], in_sems.at[d]) for d in range(STEPS)
        ]
    for copy in first:
        copy.start()
    quarter = lax.broadcasted_iota(jnp.int32, (RUN, 128), 1) // 32
    lane = lax.broadcasted_iota(jnp.int32, (PER, 128), 1)

    def taps_of(dst, d, m0):
        look_up(
            dst, lambda m: bins[d, pl.ds(m, 1), :], table[d, :, : KINDS * BINS], m0
        )

    def put(dst, m, re, im):
        dst[0, m] = re
        dst[1, m] = im
        dst[2, m] = re + im

    def halo(x):
        for m in range(PAD):
            parts = []
            for c in range(2):
                v = x[c, RUN + m]
                one = jnp.where(lane == 0, 0.0, pltpu.roll(v, 33, axis=1))
                parts.append(jnp.where(lane < 32, one, pltpu.roll(v, 32, axis=1)))
            put(x, m, *parts)
            parts = []
            for c in range(2):
                v = x[c, PAD + m]
                one = jnp.where(lane == 127, 0.0, pltpu.roll(v, 95, axis=1))
                parts.append(jnp.where(lane >= 96, one, pltpu.roll(v, 96, axis=1)))
            put(x, PAD + RUN + m, *parts)

    for c in range(2):
        for a in range(PER // 4):
            rows = [
                recv_ref[pl.ds(c * PER + 4 * a + r, GROUPS, stride=2 * PER), :] for r in range(4)
            ]
            t = jnp.concatenate(rows, axis=0).T
            for r in range(4):
                pieces = [turned(t[32 * q : 32 * q + 32], 32 * (q - r)) for q in range(4)]
                swap[c, (4 * a + r) * RUN : (4 * a + r + 1) * RUN, :] = choose(quarter, pieces)
    for m in range(RUN):
        put(xa, PAD + m, *[swap[c, pl.ds(m, PER, stride=RUN), :] for c in range(2)])
    halo(xa)
    if inline:
        for copy in first:
            copy.wait()
        for i in range(RUN // 2):
            taps_of(wa, 0, 2 * i)

    def one_step(src, dst, now, later, d):
        if not inline:
            pltpu.make_async_copy(bins_ref.at[d], held.at[d], in_sems.at[d]).wait()
        tap_rows = now if inline else held.at[d]

        def block(i, carry):
            m0 = i * MB
            if inline:
                taps_of(later, jnp.minimum(d + 1, STEPS - 1), m0)
            seen = {}

            def load(kind, row, rt):
                key = (kind, row, rt)
                if key not in seen:
                    seen[key] = src[kind, m0 + row, rt * 8 : (rt + 1) * 8, :]
                return seen[key]

            sums = {}
            for k in range(TAPS):
                for mm in range(MB):
                    taps = [
                        tap_rows[m0 + mm, pl.ds(kind * 16 + k, 8, stride=0), :]
                        for kind in range(KINDS)
                    ]
                    for rt in range(2):
                        a = load(0, mm + k, rt)
                        b = load(1, mm + k, rt)
                        s = load(2, mm + k, rt)
                        new = [taps[0] * s, taps[1] * a, taps[2] * b]
                        old = sums.get((mm, rt))
                        sums[(mm, rt)] = new if old is None else [x + y for x, y in zip(old, new)]
            for mm in range(MB):
                for rt in range(2):
                    k1, k2, k3 = sums[(mm, rt)]
                    re = k1 - k3
                    im = k1 + k2
                    at = slice(rt * 8, (rt + 1) * 8)
                    dst[0, PAD + m0 + mm, at, :] = re
                    dst[1, PAD + m0 + mm, at, :] = im
                    dst[2, PAD + m0 + mm, at, :] = re + im
            return carry

        lax.fori_loop(0, RUN // MB, block, 0, unroll=4)

    def two_steps(i, carry):
        one_step(xa, xb, wa, wb, 2 * i)
        halo(xb)
        one_step(xb, xa, wb, wa, 2 * i + 1)
        halo(xa)
        return carry

    lax.fori_loop(0, STEPS // 2, two_steps, 0)
    copies = []
    for c in range(2):
        for m in range(RUN):
            swap[c, pl.ds(m, PER, stride=RUN), :] = xa[c, PAD + m]
        for a in range(PER // 4):
            rows = [swap[c, (4 * a + r) * RUN : (4 * a + r + 1) * RUN, :] for r in range(4)]
            t = jnp.concatenate(
                [
                    choose(quarter, [turned(rows[r], 32 * (r - q)) for r in range(4)])
                    for q in range(4)
                ],
                axis=0,
            ).T
            for r in range(4):
                at = 4 * a + r
                place[c, at // 8, pl.ds(at % 8, GROUPS, stride=8), :] = t[32 * r : 32 * r + 32]
            if a % 2:
                rt = a // 2
                for i in range(GROUPS):
                    stage[c, rt, :, i * 128 : (i + 1) * 128] = place[c, rt, i * 8 : (i + 1) * 8, :]
                copy = pltpu.make_async_copy(
                    stage.at[c, rt],
                    out_ref.at[c, f, 0, rt * 8 : (rt + 1) * 8, :],
                    sems.at[c, rt],
                )
                copy.start()
                copies.append(copy)
    for copy in copies:
        copy.wait()


def src_steps(f, inline, received, bins, table, earlier=None):
    vmem = pl.BlockSpec(memory_space=pltpu.VMEM)
    flat = received.reshape(GROUPS * 2 * PER, S_DEV)
    anywhere = pl.BlockSpec(memory_space=pl.ANY)
    hbm = pl.BlockSpec(memory_space=pltpu.HBM)
    in_specs = [vmem, hbm, hbm]
    args = [flat, bins, table]
    aliases = {}
    if earlier is not None:
        in_specs.append(pl.BlockSpec(memory_space=pl.ANY))
        args.append(earlier)
        aliases = {3: 0}
    return pl.pallas_call(
        functools.partial(src_kernel, f, inline),
        out_shape=pltpu.HBM((2, F, 1, PER, NSRC), F32),
        in_specs=in_specs,
        out_specs=pl.BlockSpec(memory_space=pl.ANY),
        scratch_shapes=[
            pltpu.VMEM((KINDS, MROWS, PER, 128), F32),
            pltpu.VMEM((KINDS, MROWS, PER, 128), F32),
            pltpu.VMEM((2, PER * RUN, 128), F32),
            pltpu.VMEM((2, 2, GROUPS * 8, 128), F32),
            pltpu.VMEM((2, 2, 8, NSRC), F32),
            pltpu.SemaphoreType.DMA((2, 2)),
            pltpu.SemaphoreType.DMA((STEPS,)),
        ]
        + (
            [
                pltpu.VMEM((RUN, TROWS, 128), F32),
                pltpu.VMEM((RUN, TROWS, 128), F32),
                pltpu.VMEM((STEPS, RUN, 128), jnp.int32),
                pltpu.VMEM((STEPS, TROWS, 256), BF16),
            ]
            if inline
            else [pltpu.VMEM((STEPS, RUN, TROWS, 128), F32)]
        ),
        input_output_aliases=aliases,
        compiler_params=pltpu.CompilerParams(vmem_limit_bytes=(20 if inline else 58) * MIB),
        cost_estimate=pl.CostEstimate(
            flops=3_000_000_000, bytes_accessed=8_000_000, transcendentals=0
        ),
        name="src_steps",
    )(*args)


def shards(traces, tap_table, receiver_bins, source_bins):
    count = lax.axis_size("rcv")
    forward = [(i, i + 1) for i in range(count - 1)]
    backward = [(target, source) for source, target in forward]
    tile = lax.axis_index("rcv").astype(jnp.int32).reshape(1)
    tail = traces[:, :, :, TILE - MARGIN :].transpose(0, 1, 3, 2)
    head = traces[:, :, :, :MARGIN].transpose(0, 1, 3, 2)
    low = lax.ppermute(tail, "rcv", forward)
    high = lax.ppermute(head, "rcv", backward)
    r_taps, *local, bins, table = prepare(tile, receiver_bins, tap_table, traces, source_bins)
    sent = rcv_steps(0, local[0], low, high, r_taps)
    bins1, sent = lax.optimization_barrier((bins, sent))
    got0 = lax.all_to_all(sent, "src", split_axis=0, concat_axis=0, tiled=True)
    taps1, token = src_taps(1, bins1, table)
    sent = rcv_steps(1, local[1], low, high, r_taps, token)
    got1 = lax.all_to_all(sent, "src", split_axis=0, concat_axis=0, tiled=True)
    out = src_steps(0, True, got0, bins, table)
    return src_steps(1, False, got1, taps1, table, out)


def solution(mesh):
    in_specs = (P(None, None, "src", "rcv"), P(), P(), P())
    out_specs = P(None, None, "rcv", "src", None)
    return jax.shard_map(shards, mesh=mesh, in_specs=in_specs, out_specs=out_specs, check_vma=False)
```

```python
import functools

import jax
import jax.numpy as jnp
from jax import lax
from jax.experimental import pallas as pl
from jax.experimental.pallas import tpu as pltpu
from jax.sharding import PartitionSpec as P

F = 2
TAPS = 15
BINS = 64
STEPS = 8
HALF = 7
MARGIN = HALF * STEPS
TILE = 512
S_DEV = 128
GROUPS = 32
PER = 16
NSRC = GROUPS * S_DEV
OUTS = 112
WIN = 128
BLOCKS = 6
ROWS = 704
PCOLS = 768
RUN = 32
KINDS = 3
SPARE = 5
TROWS = 48
BF16 = jnp.bfloat16
F32 = jnp.float32
MIB = 1024 * 1024


def choose(quarter, pieces):
    out = pieces[3]
    for q in range(3):
        out = jnp.where(quarter == q, pieces[q], out)
    return out


def turned(x, shift):
    shift %= 128
    return x if shift == 0 else pltpu.roll(x, shift, axis=1)


def prepare_kernel(
    tile_ref,
    bins_ref,
    table_ref,
    local_ref,
    source_ref,
    out_ref,
    turned0_ref,
    turned1_ref,
    ordered_ref,
    split_ref,
    tiles,
):
    rows = lax.broadcasted_iota(jnp.int32, (BINS, PCOLS), 0)
    lanes = lax.broadcasted_iota(jnp.int32, (1, PCOLS), 1)
    tile = tile_ref[0]
    total = bins_ref.shape[1]
    start = tile * TILE
    before = pl.multiple_of(jnp.maximum(start - 128, 0), 128)
    after = pl.multiple_of(jnp.minimum(start + TILE, total - 128), 128)
    window = jnp.concatenate(
        [
            jnp.where(tile > 0, bins_ref[:, pl.ds(before, 128)], -1),
            bins_ref[:, pl.ds(pl.multiple_of(start, TILE), TILE)],
            jnp.where(start + TILE < total, bins_ref[:, pl.ds(after, 128)], -1),
        ],
        axis=1,
    )
    blank = jnp.zeros((1, BINS), F32)
    for d in range(STEPS):
        offset = 128 - MARGIN + HALF * (d + 1)
        row = pltpu.roll(window[d : d + 1, :], PCOLS - offset, axis=1)
        count = TILE + 2 * MARGIN - 2 * HALF * (d + 1)
        row = jnp.where(lanes < count, row, -1)
        onehot = jnp.where(rows == row, 1.0, 0.0).astype(BF16)
        parts = []
        for f in range(F):
            pair = [jnp.concatenate([table_ref[d, c, f], blank], axis=0) for c in range(2)]
            his = [x.astype(BF16) for x in pair]
            parts += his + [(x - h.astype(F32)).astype(BF16) for x, h in zip(pair, his)]
        table = jnp.concatenate(parts, axis=0)
        taps = jnp.dot(table, onehot, preferred_element_type=F32)
        for start in range(0, BLOCKS * OUTS, 128):
            size = min(128, BLOCKS * OUTS - start)
            piece = taps[:, start : start + 128].T
            out_ref[d, start : start + size, :] = piece[:size].astype(BF16)
    for f in range(F):
        for c in range(2):
            for i in range(TILE // 128):
                at = slice(i * 128, (i + 1) * 128)
                (turned0_ref, turned1_ref)[f][c, at, :] = local_ref[c, f, :, at].T
    quarter = lax.broadcasted_iota(jnp.int32, (RUN, 128), 1) // 32
    for i in range(GROUPS):
        tiles[i * 8 : (i + 1) * 8, :] = source_ref[:, i * 128 : (i + 1) * 128]
    for half in range(2):
        four = [tiles[pl.ds(4 * half + r, GROUPS, stride=8), :] for r in range(4)]
        t = jnp.concatenate(four, axis=0).T
        for r in range(4):
            pieces = [turned(t[32 * q : 32 * q + 32], 32 * (q - r)) for q in range(4)]
            ordered_ref[4 * half + r] = choose(quarter, pieces)
    unused = jnp.zeros((TROWS, 256 - 3 * BINS), BF16)
    for d in range(STEPS):
        for f in range(F):
            re, im = table_ref[d, 0, f], table_ref[d, 1, f]
            full = jnp.concatenate([re, blank, im - re, blank, re + im, blank], axis=0)
            hi = full.astype(BF16)
            rest = full - hi.astype(F32)
            mid = rest.astype(BF16)
            lo = (rest - mid.astype(F32)).astype(BF16)
            split_ref[f, d] = jnp.concatenate([hi, mid, lo, unused], axis=1)


def prepare(tile, bins, table, local, source_bins):
    vmem = pl.BlockSpec(memory_space=pltpu.VMEM)
    return pl.pallas_call(
        prepare_kernel,
        out_shape=(
            pltpu.VMEM((STEPS, BLOCKS * OUTS, 128), BF16),
            pltpu.VMEM((2, TILE, S_DEV), F32),
            pltpu.VMEM((2, TILE, S_DEV), F32),
            pltpu.HBM((STEPS, RUN, 128), jnp.int32),
            pltpu.HBM((F, STEPS, TROWS, 256), BF16),
        ),
        in_specs=[pl.BlockSpec(memory_space=pltpu.SMEM)] + [vmem] * 4,
        out_specs=(vmem,) * 5,
        scratch_shapes=[pltpu.VMEM((GROUPS * 8, 128), jnp.int32)],
        compiler_params=pltpu.CompilerParams(vmem_limit_bytes=10 * MIB),
        cost_estimate=pl.CostEstimate(flops=200_000_000, bytes_accessed=3_200_000, transcendentals=0),
        name="prepare",
    )(tile, bins, table, local, source_bins)


def put_split(dst, c, start, size, value):
    hi = value.astype(BF16)
    dst[c, start : start + size, 0:128] = hi
    dst[c, start : start + size, 128:256] = (value - hi.astype(F32)).astype(BF16)


def rcv_kernel(f, local_ref, low_ref, high_ref, taps_ref, *rest):
    out_ref, first, za, zb, last = rest[-5:]
    for c in range(2):
        first[0:MARGIN, :] = low_ref[c, f]
        first[MARGIN : MARGIN + TILE, :] = local_ref[c]
        first[MARGIN + TILE : 2 * MARGIN + TILE, :] = high_ref[c, f]
        first[2 * MARGIN + TILE :, :] = jnp.zeros((ROWS - 2 * MARGIN - TILE, 128), F32)
        for base in range(0, ROWS, 64):
            put_split(za, c, base, 64, first[base : base + 64, :])
        zb[c, BLOCKS * OUTS :, :] = jnp.zeros((ROWS - BLOCKS * OUTS, 256), BF16)

    p = lax.broadcasted_iota(jnp.int32, (OUTS, 128), 0)
    lane = lax.broadcasted_iota(jnp.int32, (OUTS, 128), 1)
    band = (lane >= p) & (lane < p + TAPS)

    def unit(src, dst, d, b, keep):
        start = b * OUTS
        w = taps_ref[d, start : start + OUTS, :].astype(F32)
        parts = []
        for kind in range(4):
            shift = (256 - 64 * f - 16 * kind) % 128
            turned = pltpu.roll(w, shift, axis=1, stride=1, stride_axis=0)
            parts.append(jnp.where(band, turned, 0.0).astype(BF16))
        re_hi, im_hi, re_lo, im_lo = parts
        lhs = jnp.concatenate(
            [
                jnp.concatenate([re_hi, -im_hi], axis=1),
                jnp.concatenate([im_hi, re_hi], axis=1),
                jnp.concatenate([re_lo, -im_lo], axis=1),
                jnp.concatenate([im_lo, re_lo], axis=1),
            ],
            axis=0,
        )
        rhs = jnp.concatenate(
            [src[0, start : start + WIN, :], src[1, start : start + WIN, :]], axis=0
        )
        product = jnp.dot(lhs, rhs, preferred_element_type=F32)
        for c in range(2):
            top = product[c * OUTS : (c + 1) * OUTS]
            low = product[(2 + c) * OUTS : (3 + c) * OUTS]
            value = top[:, :128] + (top[:, 128:] + low[:, :128])
            put_split(dst, c, start, OUTS, value)
            if keep:
                last[c, start : start + OUTS, :] = value

    def two_steps(i, blocks):
        for b in range(blocks):
            unit(za, zb, 2 * i, b, False)
        for b in range(blocks):
            unit(zb, za, 2 * i + 1, b, True)

    lax.fori_loop(0, 2, lambda i, _: (two_steps(i, BLOCKS), 0)[1], 0)
    lax.fori_loop(2, 4, lambda i, _: (two_steps(i, BLOCKS - 1), 0)[1], 0)
    for c in range(2):
        for g in range(GROUPS):
            out_ref[g, c, 0] = last[c, g * PER : (g + 1) * PER, :]


def rcv_steps(f, local, low, high, taps, *tokens):
    vmem = pl.BlockSpec(memory_space=pltpu.VMEM)
    return pl.pallas_call(
        functools.partial(rcv_kernel, f),
        out_shape=pltpu.HBM((GROUPS, 2, 1, PER, S_DEV), F32),
        in_specs=[vmem] * 4 + [pl.BlockSpec(memory_space=pl.ANY)] * len(tokens),
        out_specs=vmem,
        scratch_shapes=[
            pltpu.VMEM((ROWS, 128), F32),
            pltpu.VMEM((2, ROWS, 256), BF16),
            pltpu.VMEM((2, ROWS, 256), BF16),
            pltpu.VMEM((2, BLOCKS * OUTS, 128), F32),
        ],
        compiler_params=pltpu.CompilerParams(vmem_limit_bytes=10 * MIB),
        cost_estimate=pl.CostEstimate(
            flops=2_500_000_000, bytes_accessed=4_000_000, transcendentals=0
        ),
        name="rcv_steps",
    )(local, low, high, taps, *tokens)


def look_up(dst, row_of, table, m0):
    which = lax.broadcasted_iota(jnp.int32, (BINS, 128), 0)
    halves = []
    for h in range(2):
        onehot = jnp.where(which == row_of(m0 + h), 1.0, 0.0).astype(BF16)
        halves.append(jnp.concatenate([onehot] * 3, axis=0))
    taps = jnp.dot(table, jnp.concatenate(halves, axis=1), preferred_element_type=F32)
    for h in range(2):
        dst[m0 + h] = taps[:, h * 128 : (h + 1) * 128]


def src_taps_kernel(bins_ref, table_ref, out_ref, token_ref):
    token_ref[...] = jnp.zeros_like(token_ref)
    for i in range(RUN // 2):
        look_up(
            out_ref.at[0, 0],
            lambda m: bins_ref[0, m : m + 1, :],
            table_ref[0, 0, :, : KINDS * BINS],
            2 * i,
        )


def src_taps(f, bins, table):
    return pl.pallas_call(
        src_taps_kernel,
        grid=(STEPS,),
        out_shape=(
            pltpu.HBM((SPARE, STEPS, RUN, TROWS, 128), F32),
            pltpu.HBM((8, 128), F32),
        ),
        in_specs=[
            pl.BlockSpec((1, RUN, 128), lambda d: (d, 0, 0)),
            pl.BlockSpec((1, 1, TROWS, 256), lambda d: (f, d, 0, 0)),
        ],
        out_specs=(
            pl.BlockSpec((1, 1, RUN, TROWS, 128), lambda d: (0, d, 0, 0, 0)),
            pl.BlockSpec((8, 128), lambda d: (0, 0)),
        ),
        compiler_params=pltpu.CompilerParams(
            vmem_limit_bytes=8 * MIB, dimension_semantics=("arbitrary",)
        ),
        cost_estimate=pl.CostEstimate(
            flops=1_200_000_000, bytes_accessed=13_000_000, transcendentals=0
        ),
        name="src_taps",
    )(bins, table)


PAD = HALF
MROWS = RUN + 2 * PAD


MB = 2


NSCRATCH = {True: 12, False: 9}


def src_kernel(f, inline, recv_ref, bins_ref, table_ref, *rest):
    out_ref, xa, xb, swap, place, stage, sems, in_sems, *looked = rest[1 if len(rest) > NSCRATCH[inline] else 0 :]
    if inline:
        wa, wb, bins, table = looked
    else:
        (held,) = looked
        wa = wb = None

    if inline:
        first = [
            pltpu.make_async_copy(bins_ref, bins, in_sems.at[0]),
            pltpu.make_async_copy(table_ref.at[f], table, in_sems.at[1]),
        ]
    else:
        first = [
            pltpu.make_async_copy(bins_ref.at[0, d], held.at[d], in_sems.at[d]) for d in range(STEPS)
        ]
    for copy in first:
        copy.start()
    quarter = lax.broadcasted_iota(jnp.int32, (RUN, 128), 1) // 32
    lane = lax.broadcasted_iota(jnp.int32, (PER, 128), 1)

    def taps_of(dst, d, m0):
        look_up(
            dst, lambda m: bins[d, pl.ds(m, 1), :], table[d, :, : KINDS * BINS], m0
        )

    def put(dst, m, re, im):
        dst[0, m] = re
        dst[1, m] = im
        dst[2, m] = re + im

    def halo(x):
        for m in range(PAD):
            parts = []
            for c in range(2):
                v = x[c, RUN + m]
                one = jnp.where(lane == 0, 0.0, pltpu.roll(v, 33, axis=1))
                parts.append(jnp.where(lane < 32, one, pltpu.roll(v, 32, axis=1)))
            put(x, m, *parts)
            parts = []
            for c in range(2):
                v = x[c, PAD + m]
                one = jnp.where(lane == 127, 0.0, pltpu.roll(v, 95, axis=1))
                parts.append(jnp.where(lane >= 96, one, pltpu.roll(v, 96, axis=1)))
            put(x, PAD + RUN + m, *parts)

    for c in range(2):
        for a in range(PER // 4):
            rows = [
                recv_ref[pl.ds(c * PER + 4 * a + r, GROUPS, stride=2 * PER), :] for r in range(4)
            ]
            t = jnp.concatenate(rows, axis=0).T
            for r in range(4):
                pieces = [turned(t[32 * q : 32 * q + 32], 32 * (q - r)) for q in range(4)]
                swap[c, (4 * a + r) * RUN : (4 * a + r + 1) * RUN, :] = choose(quarter, pieces)
    for m in range(RUN):
        put(xa, PAD + m, *[swap[c, pl.ds(m, PER, stride=RUN), :] for c in range(2)])
    halo(xa)
    if inline:
        for copy in first:
            copy.wait()
        for i in range(RUN // 2):
            taps_of(wa, 0, 2 * i)

    def one_step(src, dst, now, later, d):
        if not inline:
            pltpu.make_async_copy(bins_ref.at[0, d], held.at[d], in_sems.at[d]).wait()
        tap_rows = now if inline else held.at[d]

        def block(i, carry):
            m0 = i * MB
            if inline:
                taps_of(later, jnp.minimum(d + 1, STEPS - 1), m0)
            seen = {}

            def load(kind, row, rt):
                key = (kind, row, rt)
                if key not in seen:
                    seen[key] = src[kind, m0 + row, rt * 8 : (rt + 1) * 8, :]
                return seen[key]

            sums = {}
            for k in range(TAPS):
                for mm in range(MB):
                    taps = [
                        tap_rows[m0 + mm, pl.ds(kind * 16 + k, 8, stride=0), :]
                        for kind in range(KINDS)
                    ]
                    for rt in range(2):
                        a = load(0, mm + k, rt)
                        b = load(1, mm + k, rt)
                        s = load(2, mm + k, rt)
                        new = [taps[0] * s, taps[1] * a, taps[2] * b]
                        old = sums.get((mm, rt))
                        sums[(mm, rt)] = new if old is None else [x + y for x, y in zip(old, new)]
            for mm in range(MB):
                for rt in range(2):
                    k1, k2, k3 = sums[(mm, rt)]
                    re = k1 - k3
                    im = k1 + k2
                    at = slice(rt * 8, (rt + 1) * 8)
                    dst[0, PAD + m0 + mm, at, :] = re
                    dst[1, PAD + m0 + mm, at, :] = im
                    dst[2, PAD + m0 + mm, at, :] = re + im
            return carry

        lax.fori_loop(0, RUN // MB, block, 0, unroll=RUN // MB)

    def two_steps(i, carry):
        one_step(xa, xb, wa, wb, 2 * i)
        halo(xb)
        one_step(xb, xa, wb, wa, 2 * i + 1)
        halo(xa)
        return carry

    lax.fori_loop(0, STEPS // 2, two_steps, 0)
    copies = []
    for c in range(2):
        for m in range(RUN):
            swap[c, pl.ds(m, PER, stride=RUN), :] = xa[c, PAD + m]
        for a in range(PER // 4):
            rows = [swap[c, (4 * a + r) * RUN : (4 * a + r + 1) * RUN, :] for r in range(4)]
            t = jnp.concatenate(
                [
                    choose(quarter, [turned(rows[r], 32 * (r - q)) for r in range(4)])
                    for q in range(4)
                ],
                axis=0,
            ).T
            for r in range(4):
                at = 4 * a + r
                place[c, at // 8, pl.ds(at % 8, GROUPS, stride=8), :] = t[32 * r : 32 * r + 32]
            if a % 2:
                rt = a // 2
                for i in range(GROUPS):
                    stage[c, rt, :, i * 128 : (i + 1) * 128] = place[c, rt, i * 8 : (i + 1) * 8, :]
                copy = pltpu.make_async_copy(
                    stage.at[c, rt],
                    out_ref.at[c, f, 0, rt * 8 : (rt + 1) * 8, :],
                    sems.at[c, rt],
                )
                copy.start()
                copies.append(copy)
    for copy in copies:
        copy.wait()


def src_steps(f, inline, received, bins, table, earlier=None):
    vmem = pl.BlockSpec(memory_space=pltpu.VMEM)
    flat = received.reshape(GROUPS * 2 * PER, S_DEV)
    anywhere = pl.BlockSpec(memory_space=pl.ANY)
    hbm = pl.BlockSpec(memory_space=pltpu.HBM)
    in_specs = [vmem, hbm, hbm]
    args = [flat, bins, table]
    aliases = {}
    if earlier is not None:
        in_specs.append(pl.BlockSpec(memory_space=pl.ANY))
        args.append(earlier)
        aliases = {3: 0}
    return pl.pallas_call(
        functools.partial(src_kernel, f, inline),
        out_shape=pltpu.HBM((2, F, 1, PER, NSRC), F32),
        in_specs=in_specs,
        out_specs=pl.BlockSpec(memory_space=pl.ANY),
        scratch_shapes=[
            pltpu.VMEM((KINDS, MROWS, PER, 128), F32),
            pltpu.VMEM((KINDS, MROWS, PER, 128), F32),
            pltpu.VMEM((2, PER * RUN, 128), F32),
            pltpu.VMEM((2, 2, GROUPS * 8, 128), F32),
            pltpu.VMEM((2, 2, 8, NSRC), F32),
            pltpu.SemaphoreType.DMA((2, 2)),
            pltpu.SemaphoreType.DMA((STEPS,)),
        ]
        + (
            [
                pltpu.VMEM((RUN, TROWS, 128), F32),
                pltpu.VMEM((RUN, TROWS, 128), F32),
                pltpu.VMEM((STEPS, RUN, 128), jnp.int32),
                pltpu.VMEM((STEPS, TROWS, 256), BF16),
            ]
            if inline
            else [pltpu.VMEM((STEPS, RUN, TROWS, 128), F32)]
        ),
        input_output_aliases=aliases,
        compiler_params=pltpu.CompilerParams(vmem_limit_bytes=(20 if inline else 36) * MIB),
        cost_estimate=pl.CostEstimate(
            flops=3_000_000_000, bytes_accessed=8_000_000, transcendentals=0
        ),
        name="src_steps",
    )(*args)


def shards(traces, tap_table, receiver_bins, source_bins):
    count = lax.axis_size("rcv")
    forward = [(i, i + 1) for i in range(count - 1)]
    backward = [(target, source) for source, target in forward]
    tile = lax.axis_index("rcv").astype(jnp.int32).reshape(1)
    tail = traces[:, :, :, TILE - MARGIN :].transpose(0, 1, 3, 2)
    head = traces[:, :, :, :MARGIN].transpose(0, 1, 3, 2)
    low = lax.ppermute(tail, "rcv", forward)
    high = lax.ppermute(head, "rcv", backward)
    r_taps, *local, bins, table = prepare(tile, receiver_bins, tap_table, traces, source_bins)
    sent = rcv_steps(0, local[0], low, high, r_taps)
    bins1, sent = lax.optimization_barrier((bins, sent))
    got0 = lax.all_to_all(sent, "src", split_axis=0, concat_axis=0, tiled=True)
    taps1, token = src_taps(1, bins1, table)
    sent = rcv_steps(1, local[1], low, high, r_taps, token)
    got1 = lax.all_to_all(sent, "src", split_axis=0, concat_axis=0, tiled=True)
    out = src_steps(0, True, got0, bins, table)
    return src_steps(1, False, got1, taps1, table, out)


def solution(mesh):
    in_specs = (P(None, None, "src", "rcv"), P(), P(), P())
    out_specs = P(None, None, "rcv", "src", None)
    return jax.shard_map(shards, mesh=mesh, in_specs=in_specs, out_specs=out_specs, check_vma=False)
```

```python
import functools

import jax
import jax.numpy as jnp
from jax import lax
from jax.experimental import pallas as pl
from jax.experimental.pallas import tpu as pltpu
from jax.sharding import PartitionSpec as P

F = 2
TAPS = 15
BINS = 64
STEPS = 8
HALF = 7
MARGIN = HALF * STEPS
TILE = 512
S_DEV = 128
GROUPS = 32
PER = 16
NSRC = GROUPS * S_DEV
OUTS = 112
WIN = 128
BLOCKS = 6
ROWS = 704
PCOLS = 768
RUN = 32
KINDS = 3
SPARE = 5
TROWS = 48
BF16 = jnp.bfloat16
F32 = jnp.float32
MIB = 1024 * 1024


def choose(quarter, pieces):
    out = pieces[3]
    for q in range(3):
        out = jnp.where(quarter == q, pieces[q], out)
    return out


def turned(x, shift):
    shift %= 128
    return x if shift == 0 else pltpu.roll(x, shift, axis=1)


def prepare_kernel(
    tile_ref,
    bins_ref,
    table_ref,
    local_ref,
    source_ref,
    out_ref,
    turned0_ref,
    turned1_ref,
    ordered_ref,
    split_ref,
    tiles,
):
    rows = lax.broadcasted_iota(jnp.int32, (BINS, PCOLS), 0)
    lanes = lax.broadcasted_iota(jnp.int32, (1, PCOLS), 1)
    tile = tile_ref[0]
    total = bins_ref.shape[1]
    start = tile * TILE
    before = pl.multiple_of(jnp.maximum(start - 128, 0), 128)
    after = pl.multiple_of(jnp.minimum(start + TILE, total - 128), 128)
    window = jnp.concatenate(
        [
            jnp.where(tile > 0, bins_ref[:, pl.ds(before, 128)], -1),
            bins_ref[:, pl.ds(pl.multiple_of(start, TILE), TILE)],
            jnp.where(start + TILE < total, bins_ref[:, pl.ds(after, 128)], -1),
        ],
        axis=1,
    )
    blank = jnp.zeros((1, BINS), F32)
    for d in range(STEPS):
        offset = 128 - MARGIN + HALF * (d + 1)
        row = pltpu.roll(window[d : d + 1, :], PCOLS - offset, axis=1)
        count = TILE + 2 * MARGIN - 2 * HALF * (d + 1)
        row = jnp.where(lanes < count, row, -1)
        onehot = jnp.where(rows == row, 1.0, 0.0).astype(BF16)
        parts = []
        for f in range(F):
            pair = [jnp.concatenate([table_ref[d, c, f], blank], axis=0) for c in range(2)]
            his = [x.astype(BF16) for x in pair]
            parts += his + [(x - h.astype(F32)).astype(BF16) for x, h in zip(pair, his)]
        table = jnp.concatenate(parts, axis=0)
        taps = jnp.dot(table, onehot, preferred_element_type=F32)
        for start in range(0, BLOCKS * OUTS, 128):
            size = min(128, BLOCKS * OUTS - start)
            piece = taps[:, start : start + 128].T
            out_ref[d, start : start + size, :] = piece[:size].astype(BF16)
    for f in range(F):
        for c in range(2):
            for i in range(TILE // 128):
                at = slice(i * 128, (i + 1) * 128)
                (turned0_ref, turned1_ref)[f][c, at, :] = local_ref[c, f, :, at].T
    quarter = lax.broadcasted_iota(jnp.int32, (RUN, 128), 1) // 32
    for i in range(GROUPS):
        tiles[i * 8 : (i + 1) * 8, :] = source_ref[:, i * 128 : (i + 1) * 128]
    for half in range(2):
        four = [tiles[pl.ds(4 * half + r, GROUPS, stride=8), :] for r in range(4)]
        t = jnp.concatenate(four, axis=0).T
        for r in range(4):
            pieces = [turned(t[32 * q : 32 * q + 32], 32 * (q - r)) for q in range(4)]
            ordered_ref[4 * half + r] = choose(quarter, pieces)
    unused = jnp.zeros((TROWS, 256 - 3 * BINS), BF16)
    for d in range(STEPS):
        for f in range(F):
            re, im = table_ref[d, 0, f], table_ref[d, 1, f]
            full = jnp.concatenate([re, blank, im - re, blank, re + im, blank], axis=0)
            hi = full.astype(BF16)
            rest = full - hi.astype(F32)
            mid = rest.astype(BF16)
            lo = (rest - mid.astype(F32)).astype(BF16)
            split_ref[f, d] = jnp.concatenate([hi, mid, lo, unused], axis=1)


def prepare(tile, bins, table, local, source_bins):
    vmem = pl.BlockSpec(memory_space=pltpu.VMEM)
    return pl.pallas_call(
        prepare_kernel,
        out_shape=(
            pltpu.VMEM((STEPS, BLOCKS * OUTS, 128), BF16),
            pltpu.VMEM((2, TILE, S_DEV), F32),
            pltpu.VMEM((2, TILE, S_DEV), F32),
            pltpu.HBM((STEPS, RUN, 128), jnp.int32),
            pltpu.HBM((F, STEPS, TROWS, 256), BF16),
        ),
        in_specs=[pl.BlockSpec(memory_space=pltpu.SMEM)] + [vmem] * 4,
        out_specs=(vmem,) * 5,
        scratch_shapes=[pltpu.VMEM((GROUPS * 8, 128), jnp.int32)],
        compiler_params=pltpu.CompilerParams(vmem_limit_bytes=60 * MIB),
        cost_estimate=pl.CostEstimate(flops=200_000_000, bytes_accessed=3_200_000, transcendentals=0),
        name="prepare",
    )(tile, bins, table, local, source_bins)


def put_split(dst, c, start, size, value):
    hi = value.astype(BF16)
    dst[c, start : start + size, 0:128] = hi
    dst[c, start : start + size, 128:256] = (value - hi.astype(F32)).astype(BF16)


FULL = (tuple(range(BLOCKS)), tuple(range(BLOCKS - 1)))
EDGES = ((0, 1, 4, 5), (0, 4))
INNER = (tuple(range(5)), tuple(range(4)))
INNER_FIRST = 64
INNER_OUTS = TILE - MARGIN - INNER_FIRST


def rcv_run(f, blocks, offset, taps_ref, za, zb, last):
    p = lax.broadcasted_iota(jnp.int32, (OUTS, 128), 0)
    lane = lax.broadcasted_iota(jnp.int32, (OUTS, 128), 1)
    band = (lane >= p) & (lane < p + TAPS)

    def unit(src, dst, d, b, keep):
        start = b * OUTS
        w = taps_ref[d, offset + start : offset + start + OUTS, :].astype(F32)
        parts = []
        for kind in range(4):
            shift = (256 - 64 * f - 16 * kind) % 128
            skewed = pltpu.roll(w, shift, axis=1, stride=1, stride_axis=0)
            parts.append(jnp.where(band, skewed, 0.0).astype(BF16))
        re_hi, im_hi, re_lo, im_lo = parts
        lhs = jnp.concatenate(
            [
                jnp.concatenate([re_hi, -im_hi], axis=1),
                jnp.concatenate([im_hi, re_hi], axis=1),
                jnp.concatenate([re_lo, -im_lo], axis=1),
                jnp.concatenate([im_lo, re_lo], axis=1),
            ],
            axis=0,
        )
        rhs = jnp.concatenate(
            [src[0, start : start + WIN, :], src[1, start : start + WIN, :]], axis=0
        )
        product = jnp.dot(lhs, rhs, preferred_element_type=F32)
        for c in range(2):
            top = product[c * OUTS : (c + 1) * OUTS]
            low = product[(2 + c) * OUTS : (3 + c) * OUTS]
            value = top[:, :128] + (top[:, 128:] + low[:, :128])
            put_split(dst, c, start, OUTS, value)
            if keep:
                last[c, start : start + OUTS, :] = value

    def two_steps(i, chosen):
        for b in chosen:
            unit(za, zb, 2 * i, b, False)
        for b in chosen:
            unit(zb, za, 2 * i + 1, b, True)

    lax.fori_loop(0, 2, lambda i, _: (two_steps(i, blocks[0]), 0)[1], 0)
    lax.fori_loop(2, 4, lambda i, _: (two_steps(i, blocks[1]), 0)[1], 0)


def rcv_kernel(f, blocks, local_ref, low_ref, high_ref, taps_ref, *rest):
    out_ref, first, za, zb, last = rest[-5:]
    for c in range(2):
        first[0:MARGIN, :] = low_ref[c, f]
        first[MARGIN : MARGIN + TILE, :] = local_ref[c]
        first[MARGIN + TILE : 2 * MARGIN + TILE, :] = high_ref[c, f]
        first[2 * MARGIN + TILE :, :] = jnp.zeros((ROWS - 2 * MARGIN - TILE, 128), F32)
        for base in range(0, ROWS, 64):
            put_split(za, c, base, 64, first[base : base + 64, :])
        zb[c, BLOCKS * OUTS :, :] = jnp.zeros((ROWS - BLOCKS * OUTS, 256), BF16)
        if blocks == EDGES:
            zb[c, 2 * OUTS : 2 * OUTS + 16, :] = jnp.zeros((16, 256), BF16)
    rcv_run(f, blocks, 0, taps_ref, za, zb, last)
    for c in range(2):
        for g in range(2 * GROUPS):
            r = g * 8
            at = slice(r % PER, r % PER + 8)
            if blocks == EDGES and INNER_FIRST <= r < INNER_FIRST + INNER_OUTS:
                piece = rest[0][c, r - INNER_FIRST : r - INNER_FIRST + 8, :]
            else:
                piece = last[c, r : r + 8, :]
            out_ref[r // PER, c, 0, at, :] = piece


def inner_kernel(f, local_ref, taps_ref, out_ref, za, zb, last):
    size = 5 * OUTS + 16
    held = TILE - 8
    for c in range(2):
        for base in range(0, size, 48):
            if base + 48 <= held:
                value = local_ref[c, 8 + base : 8 + base + 48, :]
            elif base < held:
                value = jnp.concatenate(
                    [local_ref[c, 8 + base : TILE, :], jnp.zeros((base + 48 - held, 128), F32)],
                    axis=0,
                )
            else:
                value = jnp.zeros((48, 128), F32)
            put_split(za, c, base, 48, value)
        zb[c, 5 * OUTS :, :] = jnp.zeros((16, 256), BF16)
    rcv_run(f, INNER, INNER_FIRST, taps_ref, za, zb, last)
    for c in range(2):
        out_ref[c] = last[c, :INNER_OUTS, :]


def rcv_inner(f, local, taps):
    vmem = pl.BlockSpec(memory_space=pltpu.VMEM)
    size = 5 * OUTS + 16
    return pl.pallas_call(
        functools.partial(inner_kernel, f),
        out_shape=pltpu.VMEM((2, INNER_OUTS, S_DEV), F32),
        in_specs=[vmem, vmem],
        out_specs=vmem,
        scratch_shapes=[
            pltpu.VMEM((2, size, 256), BF16),
            pltpu.VMEM((2, size, 256), BF16),
            pltpu.VMEM((2, 5 * OUTS, 128), F32),
        ],
        compiler_params=pltpu.CompilerParams(vmem_limit_bytes=10 * MIB),
        cost_estimate=pl.CostEstimate(
            flops=2_000_000_000, bytes_accessed=3_000_000, transcendentals=0
        ),
        name="rcv_inner",
    )(local, taps)


def rcv_steps(f, blocks, local, low, high, taps, *extra):
    vmem = pl.BlockSpec(memory_space=pltpu.VMEM)
    extra_spec = vmem if blocks == EDGES else pl.BlockSpec(memory_space=pl.ANY)
    return pl.pallas_call(
        functools.partial(rcv_kernel, f, blocks),
        out_shape=pltpu.HBM((GROUPS, 2, 1, PER, S_DEV), F32),
        in_specs=[vmem] * 4 + [extra_spec] * len(extra),
        out_specs=vmem,
        scratch_shapes=[
            pltpu.VMEM((ROWS, 128), F32),
            pltpu.VMEM((2, ROWS, 256), BF16),
            pltpu.VMEM((2, ROWS, 256), BF16),
            pltpu.VMEM((2, BLOCKS * OUTS, 128), F32),
        ],
        compiler_params=pltpu.CompilerParams(vmem_limit_bytes=10 * MIB),
        cost_estimate=pl.CostEstimate(
            flops=2_500_000_000, bytes_accessed=4_000_000, transcendentals=0
        ),
        name="rcv_steps",
    )(local, low, high, taps, *extra)


def look_up(dst, row_of, table, m0):
    which = lax.broadcasted_iota(jnp.int32, (BINS, 128), 0)
    halves = []
    for h in range(2):
        onehot = jnp.where(which == row_of(m0 + h), 1.0, 0.0).astype(BF16)
        halves.append(jnp.concatenate([onehot] * 3, axis=0))
    taps = jnp.dot(table, jnp.concatenate(halves, axis=1), preferred_element_type=F32)
    for h in range(2):
        dst[m0 + h] = taps[:, h * 128 : (h + 1) * 128]


def src_taps_kernel(bins_ref, table_ref, out_ref, token_ref):
    token_ref[...] = jnp.zeros_like(token_ref)
    for i in range(RUN // 2):
        look_up(
            out_ref.at[0, 0],
            lambda m: bins_ref[0, m : m + 1, :],
            table_ref[0, 0, :, : KINDS * BINS],
            2 * i,
        )


def src_taps(f, bins, table):
    return pl.pallas_call(
        src_taps_kernel,
        grid=(STEPS,),
        out_shape=(
            pltpu.HBM((SPARE, STEPS, RUN, TROWS, 128), F32),
            pltpu.HBM((8, 128), F32),
        ),
        in_specs=[
            pl.BlockSpec((1, RUN, 128), lambda d: (d, 0, 0)),
            pl.BlockSpec((1, 1, TROWS, 256), lambda d: (f, d, 0, 0)),
        ],
        out_specs=(
            pl.BlockSpec((1, 1, RUN, TROWS, 128), lambda d: (0, d, 0, 0, 0)),
            pl.BlockSpec((8, 128), lambda d: (0, 0)),
        ),
        compiler_params=pltpu.CompilerParams(
            vmem_limit_bytes=8 * MIB, dimension_semantics=("arbitrary",)
        ),
        cost_estimate=pl.CostEstimate(
            flops=1_200_000_000, bytes_accessed=13_000_000, transcendentals=0
        ),
        name="src_taps",
    )(bins, table)


PAD = HALF
MROWS = RUN + 2 * PAD


MB = 2


NSCRATCH = {True: 12, False: 9}


def src_kernel(f, inline, recv_ref, bins_ref, table_ref, *rest):
    out_ref, xa, xb, swap, place, stage, sems, in_sems, *looked = rest[1 if len(rest) > NSCRATCH[inline] else 0 :]
    if inline:
        wa, wb, bins, table = looked
    else:
        (held,) = looked
        wa = wb = None

    if inline:
        first = [
            pltpu.make_async_copy(bins_ref, bins, in_sems.at[0]),
            pltpu.make_async_copy(table_ref.at[f], table, in_sems.at[1]),
        ]
    else:
        first = [
            pltpu.make_async_copy(bins_ref.at[0, d], held.at[d], in_sems.at[d]) for d in range(STEPS)
        ]
    for copy in first:
        copy.start()
    quarter = lax.broadcasted_iota(jnp.int32, (RUN, 128), 1) // 32
    lane = lax.broadcasted_iota(jnp.int32, (PER, 128), 1)

    def taps_of(dst, d, m0):
        look_up(
            dst, lambda m: bins[d, pl.ds(m, 1), :], table[d, :, : KINDS * BINS], m0
        )

    def put(dst, m, re, im):
        dst[0, m] = re
        dst[1, m] = im
        dst[2, m] = re + im

    def halo(x):
        for m in range(PAD):
            parts = []
            for c in range(2):
                v = x[c, RUN + m]
                one = jnp.where(lane == 0, 0.0, pltpu.roll(v, 33, axis=1))
                parts.append(jnp.where(lane < 32, one, pltpu.roll(v, 32, axis=1)))
            put(x, m, *parts)
            parts = []
            for c in range(2):
                v = x[c, PAD + m]
                one = jnp.where(lane == 127, 0.0, pltpu.roll(v, 95, axis=1))
                parts.append(jnp.where(lane >= 96, one, pltpu.roll(v, 96, axis=1)))
            put(x, PAD + RUN + m, *parts)

    for c in range(2):
        for a in range(PER // 4):
            rows = [
                recv_ref[pl.ds(c * PER + 4 * a + r, GROUPS, stride=2 * PER), :] for r in range(4)
            ]
            t = jnp.concatenate(rows, axis=0).T
            for r in range(4):
                pieces = [turned(t[32 * q : 32 * q + 32], 32 * (q - r)) for q in range(4)]
                swap[c, (4 * a + r) * RUN : (4 * a + r + 1) * RUN, :] = choose(quarter, pieces)
    for m in range(RUN):
        put(xa, PAD + m, *[swap[c, pl.ds(m, PER, stride=RUN), :] for c in range(2)])
    halo(xa)
    if inline:
        for copy in first:
            copy.wait()
        for i in range(RUN // 2):
            taps_of(wa, 0, 2 * i)

    def one_step(src, dst, now, later, d):
        if not inline:
            pltpu.make_async_copy(bins_ref.at[0, d], held.at[d], in_sems.at[d]).wait()
        tap_rows = now if inline else held.at[d]

        def block(i, carry):
            m0 = i * MB
            if inline:
                taps_of(later, jnp.minimum(d + 1, STEPS - 1), m0)
            seen = {}

            def load(kind, row, rt):
                key = (kind, row, rt)
                if key not in seen:
                    seen[key] = src[kind, m0 + row, rt * 8 : (rt + 1) * 8, :]
                return seen[key]

            sums = {}
            for k in range(TAPS):
                for mm in range(MB):
                    taps = [
                        tap_rows[m0 + mm, pl.ds(kind * 16 + k, 8, stride=0), :]
                        for kind in range(KINDS)
                    ]
                    for rt in range(2):
                        a = load(0, mm + k, rt)
                        b = load(1, mm + k, rt)
                        s = load(2, mm + k, rt)
                        new = [taps[0] * s, taps[1] * a, taps[2] * b]
                        old = sums.get((mm, rt))
                        sums[(mm, rt)] = new if old is None else [x + y for x, y in zip(old, new)]
            for mm in range(MB):
                for rt in range(2):
                    k1, k2, k3 = sums[(mm, rt)]
                    re = k1 - k3
                    im = k1 + k2
                    at = slice(rt * 8, (rt + 1) * 8)
                    dst[0, PAD + m0 + mm, at, :] = re
                    dst[1, PAD + m0 + mm, at, :] = im
                    dst[2, PAD + m0 + mm, at, :] = re + im
            return carry

        lax.fori_loop(0, RUN // MB, block, 0, unroll=RUN // MB)

    def two_steps(i, carry):
        one_step(xa, xb, wa, wb, 2 * i)
        halo(xb)
        one_step(xb, xa, wb, wa, 2 * i + 1)
        halo(xa)
        return carry

    lax.fori_loop(0, STEPS // 2, two_steps, 0)
    copies = []
    for c in range(2):
        for m in range(RUN):
            swap[c, pl.ds(m, PER, stride=RUN), :] = xa[c, PAD + m]
        for a in range(PER // 4):
            rows = [swap[c, (4 * a + r) * RUN : (4 * a + r + 1) * RUN, :] for r in range(4)]
            t = jnp.concatenate(
                [
                    choose(quarter, [turned(rows[r], 32 * (r - q)) for r in range(4)])
                    for q in range(4)
                ],
                axis=0,
            ).T
            for r in range(4):
                at = 4 * a + r
                place[c, at // 8, pl.ds(at % 8, GROUPS, stride=8), :] = t[32 * r : 32 * r + 32]
            if a % 2:
                rt = a // 2
                for i in range(GROUPS):
                    stage[c, rt, :, i * 128 : (i + 1) * 128] = place[c, rt, i * 8 : (i + 1) * 8, :]
                copy = pltpu.make_async_copy(
                    stage.at[c, rt],
                    out_ref.at[c, f, 0, rt * 8 : (rt + 1) * 8, :],
                    sems.at[c, rt],
                )
                copy.start()
                copies.append(copy)
    for copy in copies:
        copy.wait()


def src_steps(f, inline, received, bins, table, earlier=None):
    vmem = pl.BlockSpec(memory_space=pltpu.VMEM)
    flat = received.reshape(GROUPS * 2 * PER, S_DEV)
    anywhere = pl.BlockSpec(memory_space=pl.ANY)
    hbm = pl.BlockSpec(memory_space=pltpu.HBM)
    in_specs = [vmem, hbm, hbm]
    args = [flat, bins, table]
    aliases = {}
    if earlier is not None:
        in_specs.append(pl.BlockSpec(memory_space=pl.ANY))
        args.append(earlier)
        aliases = {3: 0}
    return pl.pallas_call(
        functools.partial(src_kernel, f, inline),
        out_shape=pltpu.HBM((2, F, 1, PER, NSRC), F32),
        in_specs=in_specs,
        out_specs=pl.BlockSpec(memory_space=pl.ANY),
        scratch_shapes=[
            pltpu.VMEM((KINDS, MROWS, PER, 128), F32),
            pltpu.VMEM((KINDS, MROWS, PER, 128), F32),
            pltpu.VMEM((2, PER * RUN, 128), F32),
            pltpu.VMEM((2, 2, GROUPS * 8, 128), F32),
            pltpu.VMEM((2, 2, 8, NSRC), F32),
            pltpu.SemaphoreType.DMA((2, 2)),
            pltpu.SemaphoreType.DMA((STEPS,)),
        ]
        + (
            [
                pltpu.VMEM((RUN, TROWS, 128), F32),
                pltpu.VMEM((RUN, TROWS, 128), F32),
                pltpu.VMEM((STEPS, RUN, 128), jnp.int32),
                pltpu.VMEM((STEPS, TROWS, 256), BF16),
            ]
            if inline
            else [pltpu.VMEM((STEPS, RUN, TROWS, 128), F32)]
        ),
        input_output_aliases=aliases,
        compiler_params=pltpu.CompilerParams(vmem_limit_bytes=(20 if inline else 36) * MIB),
        cost_estimate=pl.CostEstimate(
            flops=3_000_000_000, bytes_accessed=8_000_000, transcendentals=0
        ),
        name="src_steps",
    )(*args)


def shards(traces, tap_table, receiver_bins, source_bins):
    count = lax.axis_size("rcv")
    forward = [(i, i + 1) for i in range(count - 1)]
    backward = [(target, source) for source, target in forward]
    tile = lax.axis_index("rcv").astype(jnp.int32).reshape(1)
    tail = traces[:, :, :, TILE - MARGIN :].transpose(0, 1, 3, 2)
    head = traces[:, :, :, :MARGIN].transpose(0, 1, 3, 2)
    low = lax.ppermute(tail, "rcv", forward)
    high = lax.ppermute(head, "rcv", backward)
    r_taps, *local, bins, table = prepare(tile, receiver_bins, tap_table, traces, source_bins)
    inner = rcv_inner(0, local[0], r_taps)
    sent = rcv_steps(0, EDGES, local[0], low, high, r_taps, inner)
    bins1, sent = lax.optimization_barrier((bins, sent))
    got0 = lax.all_to_all(sent, "src", split_axis=0, concat_axis=0, tiled=True)
    taps1, token = src_taps(1, bins1, table)
    sent = rcv_steps(1, FULL, local[1], low, high, r_taps, token)
    got1 = lax.all_to_all(sent, "src", split_axis=0, concat_axis=0, tiled=True)
    out = src_steps(0, True, got0, bins, table)
    return src_steps(1, False, got1, taps1, table, out)


def solution(mesh):
    in_specs = (P(None, None, "src", "rcv"), P(), P(), P())
    out_specs = P(None, None, "rcv", "src", None)
    return jax.shard_map(shards, mesh=mesh, in_specs=in_specs, out_specs=out_specs, check_vma=False)
```
